1024 devices in a mesh: section: 4 (over z_hi), expert: 16 (over y, x), replica: 16 (over z_lo, core).
Axes of the slice: x: 4, y: 4, z: 32 (z_hi: 4, z_lo: 8; z = z_hi * 8 + z_lo), core: 2. Of those that a mesh axis runs over, the one named last changes fastest.
Arguments:
- forward_tokens: bfloat16 [4, 32768, 2048], P('section', ('expert', 'replica')), may hold values from -6 to 6
- forward_routes: int32 [4, 32768, 1], P('section', ('expert', 'replica')), may hold values from 0 to 15; in each aligned block of 128 rows (0 to 127, 128 to 255, ..., all dimensions but the last counted through in order) at most 12 rows name the same one
- forward_gates: float32 [4, 32768, 1], P('section', ('expert', 'replica')), may hold values from 0.1 to 1
- backward_cotangent: bfloat16 [4, 32768, 2048], P('section', ('expert', 'replica')), may hold values from -6 to 6
- backward_routes: int32 [4, 32768, 1], P('section', ('expert', 'replica')), may hold values from 0 to 15; in each aligned block of 128 rows (0 to 127, 128 to 255, ..., all dimensions but the last counted through in order) at most 12 rows name the same one
- backward_gates: float32 [4, 32768, 1], P('section', ('expert', 'replica')), may hold values from 0.1 to 1
- saved_rows: bfloat16 [4, 16, 3072, 2048], P('section', 'expert', 'replica'), may hold values from -6 to 6
- gate_weight: bfloat16 [4, 16, 2048, 384], P('section', 'expert'), may hold values from -0.125 to 0.125
- up_weight: bfloat16 [4, 16, 2048, 384], P('section', 'expert'), may hold values from -0.125 to 0.125
- down_weight: bfloat16 [4, 16, 2048, 384], P('section', 'expert'), may hold values from -0.3125 to 0.3125
Outputs:
- forward_out: bfloat16 [4, 32768, 2048], P('section', ('expert', 'replica'))
- received_grad: bfloat16 [4, 32768, 2048], P('section', ('expert', 'replica'))
- expert_grads: bfloat16 [4, 16, 2048, 768], P('section', 'expert', 'replica')
The draws below stay inside these ranges and needn't reach their ends.
Inputs may be any that keep to these rules, and one draw needn't show every extreme that they name: `forward_routes`: each is an expert in flight. Among the rows of one device, no expert is named more than 12 times, and some expert reaches 12. `backward_routes`: each is an expert in flight. Among the rows of one device, no expert is named more than 12 times, and some expert reaches 12.
All inputs are finite; a program needn't handle non-finite values.
Results may differ from the reference program's by a relative error of at most 0.017.
Values may be sent and summed in bfloat16 or wider, within the bound.
No kernel may reach another device: no remote copies, remote signals or barrier semaphores. Data moves between devices by JAX's collectives and lax.ppermute only.
A program may use at most 64 MiB of HBM per device.

```python
import math
import jax
import jax.numpy as jnp
import numpy as np
from jax import lax

D = 2048
FF = 384
TOK_DEV = 128
TOP = 1
SECTIONS = 4
EXPERTS = 16
REPS = 16
CAP = 12
TOKENS = 32768


def raised(values, stream_key, source, target, parts, factor):
    def block_of(position):
        return (jnp.arange(values.shape[position]) // (values.shape[position] // parts)).reshape((-1,) + (1,) * (values.ndim - 1 - position))

    one_side = jax.random.permutation(stream_key, parts)[block_of(target)]
    second = (block_of(target) + parts // 2) % parts
    return jnp.where((block_of(source) == one_side) | (block_of(source) == second), factor * values, values)


def block_levels(key, dims, shards, least, high):
    factor_of, own = 1.0, jax.random.fold_in(key, 6)
    for axis_at, parts in shards:
        heights = jnp.exp(jax.random.uniform(jax.random.fold_in(own, axis_at), (parts,), jnp.float32, least / len(shards), high / len(shards)))
        factor_of = factor_of * jnp.repeat(heights, dims[axis_at] // parts).reshape([-1 if axis == axis_at else 1 for axis in range(len(dims))])
    return factor_of


def deal_out(key, own, number, rows, amount, top, reach, slope):
    order = jax.random.permutation(key, amount)
    packed, ordinary = load_shares(amount, rows * top, reach, slope, True), load_shares(amount, rows * top, reach, slope, False)
    places = jnp.arange(amount)

    def named(tallies, turn):
        used = int((tallies > 0).sum())
        fixed = max(1, used // 4)
        shifted = fixed + (places - fixed + turn * (used - fixed)) % max(1, amount - fixed)
        return jnp.zeros((amount,), jnp.int32).at[order[jnp.where(places < fixed, places, shifted)]].set(jnp.asarray(tallies, jnp.int32))

    tallies = jnp.where(number % 4 == 0, named(packed, number // 4), named(ordinary, number - number // 4 - 1))
    mixed = jax.random.permutation(jax.random.fold_in(own, 3), amount)
    giver, sink = mixed[0:amount // 2 * 2:2], mixed[1:amount // 2 * 2:2]
    margin = jnp.minimum(tallies[giver] - 1, reach - tallies[sink]) // 2
    margin = jnp.where((giver == order[0]) | (sink == order[0]) | (tallies[sink] == 0), 0, jnp.maximum(margin, 0))
    shifted = jax.random.randint(jax.random.fold_in(own, 4), (amount // 2,), 0, 1 << 20) % (margin + 1)
    tallies = tallies.at[giver].add(-shifted).at[sink].add(shifted)
    members = jnp.searchsorted(jnp.cumsum(tallies), jnp.arange(rows * top), side="right").astype(jnp.int32)
    grid = members.reshape(top, rows).T
    grid = grid[jax.random.permutation(jax.random.fold_in(own, 1), rows)]
    turn = jax.random.randint(jax.random.fold_in(own, 2), (rows, 1), 0, top)
    return jnp.take_along_axis(grid, (jnp.arange(top)[None, :] + turn) % top, axis=1)


def load_shares(number_of, total, reach, skew, full):
    loads = [(1 << 20) // math.isqrt(standing ** skew) + 1 for standing in range(1, number_of + 1)]
    largest = reach if full else min(reach, max(-(-total // number_of), total * loads[0] // sum(loads)))
    least = 1 if total - largest >= number_of - 1 else 0
    given, spare = [largest] + [least] * (number_of - 1), total - largest - least * (number_of - 1)
    while spare > 0:
        candidates = [i for i in range(1, number_of) if given[i] < largest] or [i for i in range(1, number_of) if given[i] < reach]
        pool, remaining = sum([loads[i] for i in candidates]), spare
        for i in candidates:
            more = min(reach - given[i], max(1, remaining * loads[i] // pool), spare)
            given[i] = given[i] + more
            spare = spare - more
    return np.array(given)


def centred(own_key, dims, scale, bound, split=(), held_as=jnp.bfloat16):
    values = scale * jax.random.normal(own_key, dims, jnp.float32)
    if split:
        values = values * block_levels(own_key, dims, split, -0.22, 0.18)
    return jnp.clip(values, -bound, bound).astype(held_as)


def bell_draw_with(own_key, extent, scale, most, pieces, heavy, kind=jnp.bfloat16):
    drawn = scale * jax.random.normal(own_key, extent, jnp.float32)
    if pieces:
        drawn = drawn * block_levels(own_key, extent, pieces, -0.22, 0.18)
    return jnp.clip(raised(drawn, jax.random.fold_in(own_key, 3), *heavy), -most, most).astype(kind)


def setup_inputs(seed: int = 0) -> dict:
    splits = jax.random.split(jax.random.key(seed), 11)
    forward_tokens = centred(splits[0], (SECTIONS, TOKENS, D), 1.0, 6.0, ((0, 4), (1, 256)))
    forward_routes_keys = jax.random.split(jax.random.fold_in(splits[1], 1), SECTIONS * TOKENS // TOK_DEV)
    forward_routes_turns = jax.random.permutation(jax.random.fold_in(splits[1], 3), SECTIONS * TOKENS // TOK_DEV)
    forward_routes = jax.vmap(lambda own, number: deal_out(jax.random.fold_in(splits[1], 2), own, number, TOK_DEV, EXPERTS, TOP, CAP, 2))(forward_routes_keys, forward_routes_turns).reshape((SECTIONS, TOKENS, TOP))
    forward_gates = jnp.clip(0.1 + 0.9 * jax.random.uniform(splits[2], (SECTIONS, TOKENS, TOP), jnp.float32) ** block_levels(splits[2], (SECTIONS, TOKENS, TOP), ((0, 4), (1, 256)), -0.2, 0.2), 0.1, 1.0)
    backward_cotangent = centred(splits[3], (SECTIONS, TOKENS, D), 1.0, 6.0, ((0, 4), (1, 256)))
    backward_routes_keys = jax.random.split(jax.random.fold_in(splits[4], 1), SECTIONS * TOKENS // TOK_DEV)
    backward_routes_turns = jax.random.permutation(jax.random.fold_in(splits[4], 3), SECTIONS * TOKENS // TOK_DEV)
    backward_routes = jax.vmap(lambda own, number: deal_out(jax.random.fold_in(splits[4], 2), own, number, TOK_DEV, EXPERTS, TOP, CAP, 2))(backward_routes_keys, backward_routes_turns).reshape((SECTIONS, TOKENS, TOP))
    backward_gates = jnp.clip(0.1 + 0.9 * jax.random.uniform(splits[5], (SECTIONS, TOKENS, TOP), jnp.float32) ** block_levels(splits[5], (SECTIONS, TOKENS, TOP), ((0, 4), (1, 256)), -0.2, 0.2), 0.1, 1.0)
    saved_rows = bell_draw_with(splits[6], (SECTIONS, EXPERTS, REPS * EXPERTS * CAP, D), 1.0, 6.0, ((0, 4), (1, 16), (2, 16)), (2, 3, 16, 2.0))
    gate_weight = centred(splits[7], (SECTIONS, EXPERTS, D, FF), D ** -0.5, 0.125, ((0, 4), (1, 16)))
    up_weight = centred(splits[8], (SECTIONS, EXPERTS, D, FF), D ** -0.5, 0.125, ((0, 4), (1, 16)))
    down_weight = centred(splits[9], (SECTIONS, EXPERTS, D, FF), FF ** -0.5, 0.3125, ((0, 4), (1, 16)))
    return {"forward_tokens": forward_tokens, "forward_routes": forward_routes, "forward_gates": forward_gates, "backward_cotangent": backward_cotangent, "backward_routes": backward_routes, "backward_gates": backward_gates, "saved_rows": saved_rows, "gate_weight": gate_weight, "up_weight": up_weight, "down_weight": down_weight}


def slot_tables(routes):
    blocks = routes.reshape(TOKENS // TOK_DEV, TOK_DEV * TOP)
    member = (blocks[:, :, None] == jnp.arange(EXPERTS, dtype=jnp.int32)[None, None, :]).astype(jnp.int32)
    earlier = jnp.cumsum(member, axis=1) - member
    slot_index = jnp.sum(earlier * member, axis=2).astype(jnp.int32)
    return blocks, slot_index


def dispatch(values, blocks, slot_index):
    block_count = TOKENS // TOK_DEV
    block_index = jnp.broadcast_to(jnp.arange(block_count, dtype=jnp.int32)[:, None], blocks.shape)
    buffer = jnp.zeros((block_count, EXPERTS, CAP, D), values.dtype)
    buffer = buffer.at[block_index, blocks, slot_index].add(values)
    buffer = buffer.reshape(EXPERTS, REPS, EXPERTS, CAP, D).transpose(2, 1, 0, 3, 4)
    return buffer.reshape(EXPERTS, REPS * EXPERTS * CAP, D)


def collect(row_block, blocks, slot_index):
    block_count = TOKENS // TOK_DEV
    buffer = row_block.reshape(EXPERTS, REPS, EXPERTS, CAP, D).transpose(2, 1, 0, 3, 4)
    buffer = buffer.reshape(block_count, EXPERTS, CAP, D)
    block_index = jnp.broadcast_to(jnp.arange(block_count, dtype=jnp.int32)[:, None], blocks.shape)
    return buffer[block_index, blocks, slot_index]


def expert_forward(operands):
    row_block, w_gate, w_up, w_down = operands
    gate_pre = jnp.dot(row_block, w_gate, preferred_element_type=jnp.float32)
    up_pre = jnp.dot(row_block, w_up, preferred_element_type=jnp.float32)
    hidden = (gate_pre * jax.nn.sigmoid(gate_pre) * up_pre).astype(jnp.bfloat16)
    result = lax.dot_general(hidden, w_down, (((1,), (1,)), ((), ())), preferred_element_type=jnp.float32)
    return result.astype(jnp.bfloat16)


def expert_backward(operands):
    row_block, cot_block, w_gate, w_up, w_down = operands
    gate_pre = jnp.dot(row_block, w_gate, preferred_element_type=jnp.float32)
    up_pre = jnp.dot(row_block, w_up, preferred_element_type=jnp.float32)
    sigma = jax.nn.sigmoid(gate_pre)
    hidden_grad = jnp.dot(cot_block, w_down, preferred_element_type=jnp.float32)
    up_grad = (hidden_grad * gate_pre * sigma).astype(jnp.bfloat16)
    gate_grad = (hidden_grad * up_pre * sigma * (1.0 + gate_pre * (1.0 - sigma))).astype(jnp.bfloat16)
    contract = (((1,), (1,)), ((), ()))
    row_grad = lax.dot_general(gate_grad, w_gate, contract, preferred_element_type=jnp.float32)
    row_grad = row_grad + lax.dot_general(up_grad, w_up, contract, preferred_element_type=jnp.float32)
    return row_grad.astype(jnp.bfloat16), gate_grad, up_grad


def replica_sums(row_block, gate_grad, up_grad):
    def partial_term(operands):
        part_rows, part_grads = operands
        contract = (((0,), (0,)), ((), ()))
        term = lax.dot_general(part_rows, part_grads, contract, preferred_element_type=jnp.float32)
        return term.astype(jnp.bfloat16)

    both = jnp.concatenate([gate_grad, up_grad], axis=1)
    rows_split = row_block.reshape(REPS, EXPERTS * CAP, D)
    grads_split = both.reshape(REPS, EXPERTS * CAP, 2 * FF)
    partials = lax.map(partial_term, (rows_split, grads_split))
    return jnp.sum(partials.astype(jnp.float32), axis=0).astype(jnp.bfloat16)


def section_pass(operands):
    (forward_tokens, forward_routes, forward_gates, backward_cotangent, backward_routes, backward_gates, saved_rows, gate_weight, up_weight, down_weight) = operands
    block_count = TOKENS // TOK_DEV
    blocks, slot_index = slot_tables(forward_routes)
    grouped = forward_tokens.reshape(block_count, TOK_DEV, 1, D)
    copies = jnp.broadcast_to(grouped, (block_count, TOK_DEV, TOP, D)).reshape(block_count, TOK_DEV * TOP, D)
    expert_rows = dispatch(copies, blocks, slot_index)
    outputs = lax.map(expert_forward, (expert_rows, gate_weight, up_weight, down_weight))
    returned = collect(outputs, blocks, slot_index).astype(jnp.float32)
    weighted = returned * forward_gates.reshape(block_count, TOK_DEV * TOP, 1)
    mixed = jnp.sum(weighted.reshape(TOKENS, TOP, D), axis=1)
    forward_out = (forward_tokens.astype(jnp.float32) + mixed).astype(jnp.bfloat16)

    back_blocks, back_slots = slot_tables(backward_routes)
    scaled = backward_gates.reshape(TOKENS, TOP, 1) * backward_cotangent.astype(jnp.float32)[:, None, :]
    scaled = scaled.astype(jnp.bfloat16).reshape(block_count, TOK_DEV * TOP, D)
    cot_rows = dispatch(scaled, back_blocks, back_slots)

    def per_expert(inner):
        row_block, cot_block, w_gate, w_up, w_down = inner
        row_grad, gate_grad, up_grad = expert_backward((row_block, cot_block, w_gate, w_up, w_down))
        return row_grad, replica_sums(row_block, gate_grad, up_grad)

    row_grads, weight_grads = lax.map(per_expert, (saved_rows, cot_rows, gate_weight, up_weight, down_weight))
    back = collect(row_grads, back_blocks, back_slots).astype(jnp.float32).reshape(TOKENS, TOP, D)
    local_grad = (backward_cotangent.astype(jnp.float32) + jnp.sum(back, axis=1)).astype(jnp.bfloat16)
    return forward_out, local_grad, weight_grads


def reference(forward_tokens, forward_routes, forward_gates, backward_cotangent, backward_routes, backward_gates, saved_rows, gate_weight, up_weight, down_weight):
    forward_out, local_grad, weight_grads = lax.map(section_pass, (forward_tokens, forward_routes, forward_gates, backward_cotangent, backward_routes, backward_gates, saved_rows, gate_weight, up_weight, down_weight))
    received_grad = jnp.roll(local_grad, -1, axis=0)
    return forward_out, received_grad, weight_grads
```

```python
import functools

import jax
import jax.numpy as jnp
from jax import lax
from jax.experimental import pallas as pl
from jax.experimental.pallas import tpu as pltpu
from jax.sharding import PartitionSpec as P


BF = jnp.bfloat16
F32 = jnp.float32
SLOTS = 16
COLS = 512
PLAIN = (((1,), (0,)), ((), ()))
RIGHT_T = (((1,), (1,)), ((), ()))
LEFT_T = (((0,), (0,)), ((), ()))


def dot(a, b, dims=PLAIN):
    return lax.dot_general(a, b, dims, preferred_element_type=F32)


def iota(shape, axis):
    return lax.broadcasted_iota(jnp.int32, shape, axis)


def slot_mask(ids, experts):
    tokens = ids.shape[1]
    member = iota((experts, tokens), 0) == ids
    ones = jnp.where(member, 1.0, 0.0)
    before = jnp.where(iota((tokens, tokens), 0) < iota((tokens, tokens), 1), 1.0, 0.0)
    earlier = dot(ones.astype(BF), before.astype(BF))
    slot = jnp.sum(ones * earlier, axis=0, keepdims=True).astype(jnp.int32)
    return iota((experts * SLOTS, tokens), 0) == ids * SLOTS + slot


def columns(width):
    return [slice(at, min(at + COLS, width)) for at in range(0, width, COLS)]


def write_out(held_ref, out_ref, sem_ref, fill):
    copies = []
    for k, part in enumerate(columns(out_ref.shape[1])):
        held_ref[:, part] = fill(part)
        copies.append(pltpu.make_async_copy(held_ref.at[:, part], out_ref.at[:, part], sem_ref.at[k]))
        copies[-1].start()
    for copy in copies:
        copy.wait()


def pack_kernel(experts, scaled, ids_ref, gate_ref, value_ref, out_ref, held_ref, sem_ref):
    mask = slot_mask(ids_ref[...], experts)
    table = jnp.where(mask, 1.0, 0.0).astype(BF)
    if scaled:
        gate = jnp.sum(jnp.where(mask, gate_ref[...], 0.0), axis=1, keepdims=True)

    def fill(part):
        rows = dot(table, value_ref[:, part])
        return (rows * gate if scaled else rows).astype(BF)

    write_out(held_ref, out_ref, sem_ref, fill)


def unpack_kernel(experts, scaled, ids_ref, gate_ref, value_ref, back_ref, *out_refs):
    mask = slot_mask(ids_ref[...], experts)
    table = jnp.where(mask, 1.0, 0.0).astype(BF)
    tokens = ids_ref.shape[1]
    if scaled:
        eye = iota((tokens, tokens), 0) == iota((tokens, tokens), 1)
        gate = jnp.sum(jnp.where(eye, gate_ref[...], 0.0), axis=1, keepdims=True)
    at = 0
    for out_ref in out_refs:
        for part in columns(out_ref.shape[1]):
            source = slice(at + part.start, at + part.stop)
            rows = dot(table, back_ref[:, source], LEFT_T)
            if scaled:
                rows = rows * gate
            out_ref[:, part] = (value_ref[:, source].astype(F32) + rows).astype(BF)
        at += out_ref.shape[1]


def spread_mask(experts, rows):
    capacity = rows // experts
    shape = (experts * SLOTS, rows)
    at, of = iota(shape, 0), iota(shape, 1)
    filled = at % SLOTS < capacity
    return filled & (of == at // SLOTS * capacity + at % SLOTS)


def recompute_kernel(experts, x_ref, gate_ref, up_ref, a_ref, b_ref):
    table = jnp.where(spread_mask(experts, x_ref.shape[0]), 1.0, 0.0).astype(BF)
    rows = dot(table, x_ref[...]).astype(BF)
    gate_pre = dot(rows, gate_ref[...])
    up_pre = dot(rows, up_ref[...])
    sigma = jax.nn.sigmoid(gate_pre)
    a_ref[...] = gate_pre * sigma
    b_ref[...] = up_pre * sigma * (1.0 + gate_pre * (1.0 - sigma))


def backward_kernel(
    experts, cot_ref, a_ref, b_ref, gate_ref, up_ref, down_ref, out_ref, grads_ref, held_ref, sem_ref
):
    ff = a_ref.shape[1]
    hidden_grad = dot(cot_ref[...], down_ref[...])
    gate_grad = (hidden_grad * b_ref[...]).astype(BF)
    up_grad = (hidden_grad * a_ref[...]).astype(BF)

    def fill(part):
        grad = dot(gate_grad, gate_ref[part, :], RIGHT_T)
        return (grad + dot(up_grad, up_ref[part, :], RIGHT_T)).astype(BF)

    write_out(held_ref, out_ref, sem_ref, fill)
    table = jnp.where(spread_mask(experts, grads_ref.shape[0]), 1.0, 0.0).astype(BF)
    grads_ref[:, :ff] = dot(table, gate_grad, LEFT_T).astype(BF)
    grads_ref[:, ff:] = dot(table, up_grad, LEFT_T).astype(BF)


def forward_kernel(x_ref, gate_ref, up_ref, down_ref, out_ref, held_ref, sem_ref):
    gate_pre = dot(x_ref[...], gate_ref[...])
    up_pre = dot(x_ref[...], up_ref[...])
    hidden = (gate_pre * jax.nn.sigmoid(gate_pre) * up_pre).astype(BF)

    def fill(part):
        return dot(hidden, down_ref[part, :], RIGHT_T).astype(BF)

    write_out(held_ref, out_ref, sem_ref, fill)


def call(kernel, outs, *args, scratch=(), out_first=False):
    shapes = [jax.ShapeDtypeStruct(*out) for out in outs]
    specs = [pl.BlockSpec() for _ in outs]
    if out_first:
        specs[0] = pl.BlockSpec(memory_space=pltpu.HBM)
        parts = len(columns(shapes[0].shape[1]))
        scratch = [pltpu.VMEM(*outs[0]), pltpu.SemaphoreType.DMA((parts,))]
    moved = sum(x.size * x.dtype.itemsize for x in list(args) + shapes)
    result = pl.pallas_call(
        kernel,
        out_shape=shapes,
        out_specs=specs,
        scratch_shapes=scratch,
        compiler_params=pltpu.CompilerParams(vmem_limit_bytes=16 << 20),
        cost_estimate=pl.CostEstimate(flops=0, bytes_accessed=moved, transcendentals=0),
    )(*args)
    return result[0] if len(outs) == 1 else result


def quarters_kernel(x_ref, *out_refs):
    mine = lax.rem(lax.axis_index("replica"), 4)
    for flip, out_ref in enumerate(out_refs):
        owner = mine ^ flip
        for k in range(out_ref.shape[1] // 128):
            at = pl.multiple_of((4 * k + owner) * 128, 128)
            out_ref[:, k * 128 : (k + 1) * 128] = x_ref[:, pl.ds(at, 128)]


def transpose_kernel(*refs):
    *x_refs, out_ref, cat_ref = refs
    rows = x_refs[0].shape[0]
    for k, x_ref in enumerate(x_refs):
        cat_ref[k * rows : (k + 1) * rows, :] = x_ref[...]
    for k in range(out_ref.shape[0] // 128):
        out_ref[k * 128 : (k + 1) * 128, :] = cat_ref[:, k * 128 : (k + 1) * 128].T


def partial_kernel(x_ref, *refs):
    *grad_refs, keep_ref, send_ref, cat_ref = refs
    rows = grad_refs[0].shape[0]
    for k, grad_ref in enumerate(grad_refs):
        cat_ref[k * rows : (k + 1) * rows, :] = grad_ref[...]
    bit = lax.rem(lax.axis_index("replica") // 4, 2)
    for half in range(2):
        part = slice(half * 128, (half + 1) * 128)
        at = pl.multiple_of((2 * half + bit) * 128, 128)
        keep_ref[part, :] = dot(x_ref[pl.ds(at, 128), :], cat_ref[...])
        at = pl.multiple_of((2 * half + 1 - bit) * 128, 128)
        send_ref[part, :] = dot(x_ref[pl.ds(at, 128), :], cat_ref[...]).astype(BF)


def halve_kernel(keep_ref, got_ref, kept_ref, send_ref):
    bit = lax.axis_index("replica") // 8
    at = pl.ds(pl.multiple_of(bit * 128, 128), 128)
    kept_ref[...] = keep_ref[at, :] + got_ref[at, :].astype(F32)
    at = pl.ds(pl.multiple_of((1 - bit) * 128, 128), 128)
    send_ref[...] = (keep_ref[at, :] + got_ref[at, :].astype(F32)).astype(BF)


def last_kernel(keep_ref, got_ref, out_ref):
    out_ref[...] = (keep_ref[...] + got_ref[...].astype(F32)).astype(BF)


def swap(value, bit):
    count = lax.axis_size("replica")
    return lax.ppermute(value, "replica", [(at, at ^ bit) for at in range(count)])


def turn(value, steps):
    count = lax.axis_size("section")
    return lax.ppermute(value, "section", [(at, (at + steps) % count) for at in range(count)])


def exchange(rows):
    experts = lax.axis_size("expert")
    blocks = rows.reshape(experts, SLOTS, rows.shape[1])
    got = lax.all_to_all(blocks, "expert", 0, 0, tiled=True)
    return got.reshape(rows.shape)


def shards(
    forward_tokens,
    forward_routes,
    forward_gates,
    backward_cotangent,
    backward_routes,
    backward_gates,
    saved_rows,
    gate_weight,
    up_weight,
    down_weight,
):
    experts = lax.axis_size("expert")
    x = saved_rows[0, 0]
    rows, width = x.shape
    w_gate, w_up, w_down = gate_weight[0, 0], up_weight[0, 0], down_weight[0, 0]
    ff = w_gate.shape[1]
    tokens, cot = forward_tokens[0], backward_cotangent[0]
    count = tokens.shape[0]
    f_ids, b_ids = forward_routes.reshape(1, count), backward_routes.reshape(1, count)
    f_gate, b_gate = forward_gates.reshape(1, count), backward_gates.reshape(1, count)
    slots = experts * SLOTS
    first = width * 3 // 16
    part = functools.partial
    blocks = ((slots, width), BF)

    packed = call(part(pack_kernel, experts, True), [blocks], b_ids, b_gate, cot, out_first=True)
    cot_rows = exchange(packed)
    a, b = call(part(recompute_kernel, experts), [((slots, ff), F32)] * 2, x, w_gate, w_up)
    own, *others = call(quarters_kernel, [((rows, width // 4), BF)] * 4, x)
    others = [swap(other, flip + 1) for flip, other in enumerate(others)]
    x_t = call(
        transpose_kernel, [((width // 4, 4 * rows), BF)], own, others[1], others[0], others[2],
        scratch=[pltpu.VMEM((4 * rows, width // 4), BF)],
    )
    back, grads = call(
        part(backward_kernel, experts), [blocks, ((rows, 2 * ff), BF)],
        cot_rows, a, b, w_gate, w_up, w_down, out_first=True,
    )
    back = exchange(back)

    near = [grads, swap(grads, 2)]
    keep, send = call(
        partial_kernel, [((width // 8, 2 * ff), F32), ((width // 8, 2 * ff), BF)],
        x_t, *near, swap(near[0], 1), swap(near[1], 1),
        scratch=[pltpu.VMEM((4 * rows, 2 * ff), BF)],
    )
    kept, send = call(
        halve_kernel, [((width // 16, 2 * ff), F32), ((width // 16, 2 * ff), BF)],
        keep, swap(send, 4),
    )
    weight_grads = call(last_kernel, [((width // 16, 2 * ff), BF)], kept, swap(send, 8))

    local_1, local_2 = call(
        part(unpack_kernel, experts, False), [((count, first), BF), ((count, width - first), BF)],
        b_ids, b_gate, cot, back,
    )
    received_1 = turn(turn(turn(local_1, 1), 1), 1)
    received_2 = turn(local_2, -1)
    received = jnp.concatenate([received_1, received_2], axis=1)

    f_packed = call(part(pack_kernel, experts, False), [blocks], f_ids, f_gate, tokens, out_first=True)
    f_rows = exchange(f_packed)
    f_out = call(forward_kernel, [blocks], f_rows, w_gate, w_up, w_down, out_first=True)
    f_back = exchange(f_out)
    forward_out = call(part(unpack_kernel, experts, True), [((count, width), BF)], f_ids, f_gate, tokens, f_back)
    return forward_out[None], received[None], weight_grads[None, None]


def solution(mesh):
    token = P("section", ("expert", "replica"), None)
    weight = P("section", "expert", None, None)
    row = P("section", "expert", "replica", None)
    return jax.shard_map(
        shards,
        mesh=mesh,
        in_specs=(token,) * 6 + (row,) + (weight,) * 3,
        out_specs=(token, token, row),
        check_vma=False,
    )
```

```python
import functools

import jax
import jax.numpy as jnp
from jax import lax
from jax.experimental import pallas as pl
from jax.experimental.pallas import tpu as pltpu
from jax.sharding import PartitionSpec as P


BF = jnp.bfloat16
F32 = jnp.float32
SLOTS = 16
COLS = 512
PLAIN = (((1,), (0,)), ((), ()))
RIGHT_T = (((1,), (1,)), ((), ()))
LEFT_T = (((0,), (0,)), ((), ()))


def dot(a, b, dims=PLAIN):
    return lax.dot_general(a, b, dims, preferred_element_type=F32)


def iota(shape, axis):
    return lax.broadcasted_iota(jnp.int32, shape, axis)


def slot_mask(ids, experts):
    tokens = ids.shape[1]
    member = iota((experts, tokens), 0) == ids
    ones = jnp.where(member, 1.0, 0.0)
    before = jnp.where(iota((tokens, tokens), 0) < iota((tokens, tokens), 1), 1.0, 0.0)
    earlier = dot(ones.astype(BF), before.astype(BF))
    slot = jnp.sum(ones * earlier, axis=0, keepdims=True).astype(jnp.int32)
    return iota((experts * SLOTS, tokens), 0) == ids * SLOTS + slot


def columns(width):
    return [slice(at, min(at + COLS, width)) for at in range(0, width, COLS)]


def write_out(held_ref, out_ref, sem_ref, fill):
    copies = []
    for k, part in enumerate(columns(out_ref.shape[1])):
        held_ref[:, part] = fill(part)
        copies.append(pltpu.make_async_copy(held_ref.at[:, part], out_ref.at[:, part], sem_ref.at[k]))
        copies[-1].start()
    for copy in copies:
        copy.wait()


def pack_kernel(experts, scaled, ids_ref, gate_ref, value_ref, out_ref, held_ref, sem_ref):
    mask = slot_mask(ids_ref[...], experts)
    table = jnp.where(mask, 1.0, 0.0).astype(BF)
    if scaled:
        gate = jnp.sum(jnp.where(mask, gate_ref[...], 0.0), axis=1, keepdims=True)

    def fill(part):
        rows = dot(table, value_ref[:, part])
        return (rows * gate if scaled else rows).astype(BF)

    write_out(held_ref, out_ref, sem_ref, fill)


def unpack_kernel(experts, scaled, ids_ref, gate_ref, value_ref, back_ref, *out_refs):
    mask = slot_mask(ids_ref[...], experts)
    table = jnp.where(mask, 1.0, 0.0).astype(BF)
    tokens = ids_ref.shape[1]
    if scaled:
        eye = iota((tokens, tokens), 0) == iota((tokens, tokens), 1)
        gate = jnp.sum(jnp.where(eye, gate_ref[...], 0.0), axis=1, keepdims=True)
    at = 0
    for out_ref in out_refs:
        for part in columns(out_ref.shape[1]):
            source = slice(at + part.start, at + part.stop)
            rows = dot(table, back_ref[:, source], LEFT_T)
            if scaled:
                rows = rows * gate
            out_ref[:, part] = (value_ref[:, source].astype(F32) + rows).astype(BF)
        at += out_ref.shape[1]


def spread_mask(experts, rows):
    capacity = rows // experts
    shape = (experts * SLOTS, rows)
    at, of = iota(shape, 0), iota(shape, 1)
    filled = at % SLOTS < capacity
    return filled & (of == at // SLOTS * capacity + at % SLOTS)


def recompute_kernel(experts, x_ref, gate_ref, up_ref, factors_ref):
    ff = gate_ref.shape[1]
    table = jnp.where(spread_mask(experts, x_ref.shape[0]), 1.0, 0.0).astype(BF)
    rows = dot(table, x_ref[...]).astype(BF)
    gate_pre = dot(rows, gate_ref[...])
    up_pre = dot(rows, up_ref[...])
    sigma = jax.nn.sigmoid(gate_pre)
    factors_ref[:, ff:] = gate_pre * sigma
    factors_ref[:, :ff] = up_pre * sigma * (1.0 + gate_pre * (1.0 - sigma))


def backward_kernel(experts, *refs):
    sources, (out_ref, grads_ref, held_ref, sem_ref), (*inputs, in_sem_ref) = refs[:5], refs[5:9], refs[9:]
    fetches = [
        pltpu.make_async_copy(source, held, in_sem_ref.at[k])
        for k, (source, held) in enumerate(zip(sources, inputs))
    ]
    for fetch in fetches:
        fetch.start()
    down_ref, cot_ref, factors_ref, gate_ref, up_ref = inputs
    ff = gate_ref.shape[1]
    fetches[0].wait()
    fetches[1].wait()
    hidden_grad = dot(cot_ref[...], down_ref[...])
    fetches[2].wait()
    gate_grad = (hidden_grad * factors_ref[:, :ff]).astype(BF)
    up_grad = (hidden_grad * factors_ref[:, ff:]).astype(BF)
    table = jnp.where(spread_mask(experts, grads_ref.shape[0]), 1.0, 0.0).astype(BF)
    grads_ref[:, :ff] = dot(table, gate_grad, LEFT_T).astype(BF)
    grads_ref[:, ff:] = dot(table, up_grad, LEFT_T).astype(BF)
    fetches[3].wait()
    fetches[4].wait()

    def fill(part):
        grad = dot(gate_grad, gate_ref[part, :], RIGHT_T)
        return (grad + dot(up_grad, up_ref[part, :], RIGHT_T)).astype(BF)

    write_out(held_ref, out_ref, sem_ref, fill)


def forward_kernel(x_ref, gate_ref, up_ref, down_ref, out_ref, held_ref, sem_ref):
    gate_pre = dot(x_ref[...], gate_ref[...])
    up_pre = dot(x_ref[...], up_ref[...])
    hidden = (gate_pre * jax.nn.sigmoid(gate_pre) * up_pre).astype(BF)

    def fill(part):
        return dot(hidden, down_ref[part, :], RIGHT_T).astype(BF)

    write_out(held_ref, out_ref, sem_ref, fill)


def call(kernel, outs, *args, scratch=(), out_first=False, own_fetch=False, in_hbm=False):
    in_hbm = in_hbm or out_first
    shapes = [jax.ShapeDtypeStruct(*out) for out in outs]
    specs = [pl.BlockSpec() for _ in outs]
    if out_first:
        specs[0] = pl.BlockSpec(memory_space=pltpu.HBM)
        parts = len(columns(shapes[0].shape[1]))
        scratch = [pltpu.VMEM(*outs[0]), pltpu.SemaphoreType.DMA((parts,))]
    in_specs = [pl.BlockSpec(memory_space=pltpu.HBM) if own_fetch else pl.BlockSpec() for _ in args]
    if own_fetch:
        scratch += [pltpu.VMEM(x.shape, x.dtype) for x in args] + [pltpu.SemaphoreType.DMA((len(args),))]
    moved = sum(x.size * x.dtype.itemsize for x in list(args) + shapes)
    result = pl.pallas_call(
        kernel,
        out_shape=shapes,
        in_specs=in_specs,
        out_specs=specs,
        scratch_shapes=scratch,
        compiler_params=pltpu.CompilerParams(**({} if in_hbm else {"vmem_limit_bytes": 16 << 20})),
        cost_estimate=pl.CostEstimate(flops=0, bytes_accessed=moved, transcendentals=0),
    )(*args)
    return result[0] if len(outs) == 1 else result


def quarters_kernel(x_ref, *out_refs):
    mine = lax.rem(lax.axis_index("replica"), 4)
    for flip, out_ref in enumerate(out_refs):
        owner = mine ^ flip
        for k in range(out_ref.shape[1] // 128):
            at = pl.multiple_of((4 * k + owner) * 128, 128)
            out_ref[:, k * 128 : (k + 1) * 128] = x_ref[:, pl.ds(at, 128)]


def transpose_kernel(*refs):
    *x_refs, out_ref, cat_ref = refs
    rows = x_refs[0].shape[0]
    for k, x_ref in enumerate(x_refs):
        cat_ref[k * rows : (k + 1) * rows, :] = x_ref[...]
    for k in range(out_ref.shape[0] // 128):
        out_ref[k * 128 : (k + 1) * 128, :] = cat_ref[:, k * 128 : (k + 1) * 128].T


def partial_kernel(x_ref, *refs):
    *grad_refs, keep_ref, send_ref, cat_ref = refs
    rows = grad_refs[0].shape[0]
    for k, grad_ref in enumerate(grad_refs):
        cat_ref[k * rows : (k + 1) * rows, :] = grad_ref[...]
    bit = lax.rem(lax.axis_index("replica") // 4, 2)
    for half in range(2):
        part = slice(half * 128, (half + 1) * 128)
        at = pl.multiple_of((2 * half + bit) * 128, 128)
        keep_ref[part, :] = dot(x_ref[pl.ds(at, 128), :], cat_ref[...])
        at = pl.multiple_of((2 * half + 1 - bit) * 128, 128)
        send_ref[part, :] = dot(x_ref[pl.ds(at, 128), :], cat_ref[...]).astype(BF)


def halve_kernel(keep_ref, got_ref, kept_ref, send_ref):
    bit = lax.axis_index("replica") // 8
    at = pl.ds(pl.multiple_of(bit * 128, 128), 128)
    kept_ref[...] = keep_ref[at, :] + got_ref[at, :].astype(F32)
    at = pl.ds(pl.multiple_of((1 - bit) * 128, 128), 128)
    send_ref[...] = (keep_ref[at, :] + got_ref[at, :].astype(F32)).astype(BF)


def last_kernel(keep_ref, got_ref, out_ref):
    out_ref[...] = (keep_ref[...] + got_ref[...].astype(F32)).astype(BF)


def swap(value, bit):
    count = lax.axis_size("replica")
    return lax.ppermute(value, "replica", [(at, at ^ bit) for at in range(count)])


def turn(value, steps):
    count = lax.axis_size("section")
    return lax.ppermute(value, "section", [(at, (at + steps) % count) for at in range(count)])


def exchange(rows):
    experts = lax.axis_size("expert")
    blocks = rows.reshape(experts, SLOTS, rows.shape[1])
    got = lax.all_to_all(blocks, "expert", 0, 0, tiled=True)
    return got.reshape(rows.shape)


def shards(
    forward_tokens,
    forward_routes,
    forward_gates,
    backward_cotangent,
    backward_routes,
    backward_gates,
    saved_rows,
    gate_weight,
    up_weight,
    down_weight,
):
    experts = lax.axis_size("expert")
    x = saved_rows[0, 0]
    rows, width = x.shape
    w_gate, w_up, w_down = gate_weight[0, 0], up_weight[0, 0], down_weight[0, 0]
    ff = w_gate.shape[1]
    tokens, cot = forward_tokens[0], backward_cotangent[0]
    count = tokens.shape[0]
    f_ids, b_ids = forward_routes.reshape(1, count), backward_routes.reshape(1, count)
    f_gate, b_gate = forward_gates.reshape(1, count), backward_gates.reshape(1, count)
    slots = experts * SLOTS
    first = width * 3 // 16
    part = functools.partial
    blocks = ((slots, width), BF)

    packed = call(part(pack_kernel, experts, True), [blocks], b_ids, b_gate, cot, out_first=True)
    cot_rows = exchange(packed)
    factors = call(part(recompute_kernel, experts), [((slots, 2 * ff), F32)], x, w_gate, w_up)
    own, *others = call(quarters_kernel, [((rows, width // 4), BF)] * 4, x, in_hbm=True)
    others = [swap(other, flip + 1) for flip, other in enumerate(others)]
    x_t = call(
        transpose_kernel, [((width // 4, 4 * rows), BF)], own, others[1], others[0], others[2],
        scratch=[pltpu.VMEM((4 * rows, width // 4), BF)], in_hbm=True,
    )
    back, grads = call(
        part(backward_kernel, experts), [blocks, ((rows, 2 * ff), BF)],
        w_down, cot_rows, factors, w_gate, w_up, out_first=True, own_fetch=True,
    )
    back = exchange(back)

    near = [grads, swap(grads, 2)]
    keep, send = call(
        partial_kernel, [((width // 8, 2 * ff), F32), ((width // 8, 2 * ff), BF)],
        x_t, *near, swap(near[0], 1), swap(near[1], 1),
        scratch=[pltpu.VMEM((4 * rows, 2 * ff), BF)],
    )
    kept, send = call(
        halve_kernel, [((width // 16, 2 * ff), F32), ((width // 16, 2 * ff), BF)],
        keep, swap(send, 4),
    )
    weight_grads = call(last_kernel, [((width // 16, 2 * ff), BF)], kept, swap(send, 8))

    widths = (first, (width - first) // 2, (width - first) // 2)
    local = call(
        part(unpack_kernel, experts, False), [((count, some), BF) for some in widths],
        b_ids, b_gate, cot, back,
    )
    received = [turn(turn(turn(local[0], 1), 1), 1)]
    received += [turn(local[k], -1) for k in (1, 2)]
    received = jnp.concatenate(received, axis=1)

    f_packed = call(part(pack_kernel, experts, False), [blocks], f_ids, f_gate, tokens, out_first=True)
    f_rows = exchange(f_packed)
    f_out = call(forward_kernel, [blocks], f_rows, w_gate, w_up, w_down, out_first=True)
    f_back = exchange(f_out)
    forward_out = call(part(unpack_kernel, experts, True), [((count, width), BF)], f_ids, f_gate, tokens, f_back)
    return forward_out[None], received[None], weight_grads[None, None]


def solution(mesh):
    token = P("section", ("expert", "replica"), None)
    weight = P("section", "expert", None, None)
    row = P("section", "expert", "replica", None)
    return jax.shard_map(
        shards,
        mesh=mesh,
        in_specs=(token,) * 6 + (row,) + (weight,) * 3,
        out_specs=(token, token, row),
        check_vma=False,
    )
```

```python
import functools

import jax
import jax.numpy as jnp
from jax import lax
from jax.experimental import pallas as pl
from jax.experimental.pallas import tpu as pltpu
from jax.sharding import PartitionSpec as P


BF = jnp.bfloat16
F32 = jnp.float32
SLOTS = 16
COLS = 512
PLAIN = (((1,), (0,)), ((), ()))
RIGHT_T = (((1,), (1,)), ((), ()))
LEFT_T = (((0,), (0,)), ((), ()))


def dot(a, b, dims=PLAIN):
    return lax.dot_general(a, b, dims, preferred_element_type=F32)


def iota(shape, axis):
    return lax.broadcasted_iota(jnp.int32, shape, axis)


def slot_mask(ids, experts):
    tokens = ids.shape[1]
    member = iota((experts, tokens), 0) == ids
    ones = jnp.where(member, 1.0, 0.0)
    before = jnp.where(iota((tokens, tokens), 0) < iota((tokens, tokens), 1), 1.0, 0.0)
    earlier = dot(ones.astype(BF), before.astype(BF))
    slot = jnp.sum(ones * earlier, axis=0, keepdims=True).astype(jnp.int32)
    return iota((experts * SLOTS, tokens), 0) == ids * SLOTS + slot


def columns(width):
    return [slice(at, min(at + COLS, width)) for at in range(0, width, COLS)]


def write_out(held_ref, out_ref, sem_ref, fill):
    copies = []
    for k, part in enumerate(columns(out_ref.shape[1])):
        held_ref[:, part] = fill(part)
        copies.append(pltpu.make_async_copy(held_ref.at[:, part], out_ref.at[:, part], sem_ref.at[k]))
        copies[-1].start()
    for copy in copies:
        copy.wait()


def pack_kernel(experts, scaled, ids_ref, gate_ref, value_ref, out_ref, held_ref, sem_ref):
    mask = slot_mask(ids_ref[...], experts)
    table = jnp.where(mask, 1.0, 0.0).astype(BF)
    if scaled:
        gate = jnp.sum(jnp.where(mask, gate_ref[...], 0.0), axis=1, keepdims=True)

    def fill(part):
        rows = dot(table, value_ref[:, part])
        return (rows * gate if scaled else rows).astype(BF)

    write_out(held_ref, out_ref, sem_ref, fill)


def unpack_kernel(experts, scaled, ids_ref, gate_ref, value_ref, back_ref, *out_refs):
    mask = slot_mask(ids_ref[...], experts)
    table = jnp.where(mask, 1.0, 0.0).astype(BF)
    tokens = ids_ref.shape[1]
    if scaled:
        eye = iota((tokens, tokens), 0) == iota((tokens, tokens), 1)
        gate = jnp.sum(jnp.where(eye, gate_ref[...], 0.0), axis=1, keepdims=True)
    at = 0
    for out_ref in out_refs:
        for part in columns(out_ref.shape[1]):
            source = slice(at + part.start, at + part.stop)
            rows = dot(table, back_ref[:, source], LEFT_T)
            if scaled:
                rows = rows * gate
            out_ref[:, part] = (value_ref[:, source].astype(F32) + rows).astype(BF)
        at += out_ref.shape[1]


def spread_mask(experts, rows):
    capacity = rows // experts
    shape = (experts * SLOTS, rows)
    at, of = iota(shape, 0), iota(shape, 1)
    filled = at % SLOTS < capacity
    return filled & (of == at // SLOTS * capacity + at % SLOTS)


def recompute_kernel(experts, x_ref, gate_ref, up_ref, factors_ref):
    ff = gate_ref.shape[1]
    table = jnp.where(spread_mask(experts, x_ref.shape[0]), 1.0, 0.0).astype(BF)
    rows = dot(table, x_ref[...]).astype(BF)
    gate_pre = dot(rows, gate_ref[...])
    up_pre = dot(rows, up_ref[...])
    sigma = jax.nn.sigmoid(gate_pre)
    factors_ref[:, ff:] = gate_pre * sigma
    factors_ref[:, :ff] = up_pre * sigma * (1.0 + gate_pre * (1.0 - sigma))


def backward_kernel(experts, *refs):
    sources, (out_ref, grads_ref, held_ref, sem_ref), (*inputs, in_sem_ref) = refs[:5], refs[5:9], refs[9:]
    fetches = [
        pltpu.make_async_copy(source, held, in_sem_ref.at[k])
        for k, (source, held) in enumerate(zip(sources, inputs))
    ]
    for fetch in fetches:
        fetch.start()
    down_ref, cot_ref, factors_ref, gate_ref, up_ref = inputs
    ff = gate_ref.shape[1]
    fetches[0].wait()
    fetches[1].wait()
    hidden_grad = dot(cot_ref[...], down_ref[...])
    fetches[2].wait()
    gate_grad = (hidden_grad * factors_ref[:, :ff]).astype(BF)
    up_grad = (hidden_grad * factors_ref[:, ff:]).astype(BF)
    table = jnp.where(spread_mask(experts, grads_ref.shape[0]), 1.0, 0.0).astype(BF)
    grads_ref[:, :ff] = dot(table, gate_grad, LEFT_T).astype(BF)
    grads_ref[:, ff:] = dot(table, up_grad, LEFT_T).astype(BF)
    fetches[3].wait()
    fetches[4].wait()

    def fill(part):
        grad = dot(gate_grad, gate_ref[part, :], RIGHT_T)
        return (grad + dot(up_grad, up_ref[part, :], RIGHT_T)).astype(BF)

    write_out(held_ref, out_ref, sem_ref, fill)


def forward_kernel(x_ref, gate_ref, up_ref, down_ref, out_ref, held_ref, sem_ref):
    gate_pre = dot(x_ref[...], gate_ref[...])
    up_pre = dot(x_ref[...], up_ref[...])
    hidden = (gate_pre * jax.nn.sigmoid(gate_pre) * up_pre).astype(BF)

    def fill(part):
        return dot(hidden, down_ref[part, :], RIGHT_T).astype(BF)

    write_out(held_ref, out_ref, sem_ref, fill)


def call(kernel, outs, *args, scratch=(), out_first=False, own_fetch=False, in_hbm=False):
    in_hbm = in_hbm or out_first
    shapes = [jax.ShapeDtypeStruct(*out) for out in outs]
    specs = [pl.BlockSpec() for _ in outs]
    if out_first:
        specs[0] = pl.BlockSpec(memory_space=pltpu.HBM)
        parts = len(columns(shapes[0].shape[1]))
        scratch = [pltpu.VMEM(*outs[0]), pltpu.SemaphoreType.DMA((parts,))]
    in_specs = [pl.BlockSpec(memory_space=pltpu.HBM) if own_fetch else pl.BlockSpec() for _ in args]
    if own_fetch:
        scratch += [pltpu.VMEM(x.shape, x.dtype) for x in args] + [pltpu.SemaphoreType.DMA((len(args),))]
    moved = sum(x.size * x.dtype.itemsize for x in list(args) + shapes)
    result = pl.pallas_call(
        kernel,
        out_shape=shapes,
        in_specs=in_specs,
        out_specs=specs,
        scratch_shapes=scratch,
        compiler_params=pltpu.CompilerParams(**({} if in_hbm else {"vmem_limit_bytes": 16 << 20})),
        cost_estimate=pl.CostEstimate(flops=0, bytes_accessed=moved, transcendentals=0),
    )(*args)
    return result[0] if len(outs) == 1 else result


def quarters_kernel(x_ref, *out_refs):
    mine = lax.rem(lax.axis_index("replica"), 4)
    for flip, out_ref in enumerate(out_refs):
        owner = mine ^ flip
        for k in range(out_ref.shape[1] // 128):
            at = pl.multiple_of((4 * k + owner) * 128, 128)
            out_ref[:, k * 128 : (k + 1) * 128] = x_ref[:, pl.ds(at, 128)]


def transpose_kernel(*refs):
    *x_refs, out_ref, cat_ref = refs
    rows = x_refs[0].shape[0]
    for k, x_ref in enumerate(x_refs):
        cat_ref[k * rows : (k + 1) * rows, :] = x_ref[...]
    for k in range(out_ref.shape[0] // 128):
        out_ref[k * 128 : (k + 1) * 128, :] = cat_ref[:, k * 128 : (k + 1) * 128].T


def partial_kernel(x_ref, *refs):
    *grad_refs, keep_ref, send_ref, cat_ref = refs
    rows = grad_refs[0].shape[0]
    for k, grad_ref in enumerate(grad_refs):
        cat_ref[k * rows : (k + 1) * rows, :] = grad_ref[...]
    bit = lax.rem(lax.axis_index("replica") // 4, 2)
    for half in range(2):
        part = slice(half * 128, (half + 1) * 128)
        at = pl.multiple_of((2 * half + bit) * 128, 128)
        keep_ref[part, :] = dot(x_ref[pl.ds(at, 128), :], cat_ref[...])
        at = pl.multiple_of((2 * half + 1 - bit) * 128, 128)
        send_ref[part, :] = dot(x_ref[pl.ds(at, 128), :], cat_ref[...]).astype(BF)


def halve_kernel(keep_ref, got_ref, kept_ref, send_ref):
    bit = lax.axis_index("replica") // 8
    at = pl.ds(pl.multiple_of(bit * 128, 128), 128)
    kept_ref[...] = keep_ref[at, :] + got_ref[at, :].astype(F32)
    at = pl.ds(pl.multiple_of((1 - bit) * 128, 128), 128)
    send_ref[...] = (keep_ref[at, :] + got_ref[at, :].astype(F32)).astype(BF)


def last_kernel(keep_ref, got_ref, out_ref):
    out_ref[...] = (keep_ref[...] + got_ref[...].astype(F32)).astype(BF)


def join_kernel(*refs):
    *part_refs, out_ref = refs
    at = 0
    for part_ref in part_refs:
        out_ref[:, at : at + part_ref.shape[1]] = part_ref[...]
        at += part_ref.shape[1]


def swap(value, bit):
    count = lax.axis_size("replica")
    return lax.ppermute(value, "replica", [(at, at ^ bit) for at in range(count)])


def turn(value, steps):
    count = lax.axis_size("section")
    return lax.ppermute(value, "section", [(at, (at + steps) % count) for at in range(count)])


def exchange(rows):
    experts = lax.axis_size("expert")
    blocks = rows.reshape(experts, SLOTS, rows.shape[1])
    got = lax.all_to_all(blocks, "expert", 0, 0, tiled=True)
    return got.reshape(rows.shape)


def shards(
    forward_tokens,
    forward_routes,
    forward_gates,
    backward_cotangent,
    backward_routes,
    backward_gates,
    saved_rows,
    gate_weight,
    up_weight,
    down_weight,
):
    experts = lax.axis_size("expert")
    x = saved_rows[0, 0]
    rows, width = x.shape
    w_gate, w_up, w_down = gate_weight[0, 0], up_weight[0, 0], down_weight[0, 0]
    ff = w_gate.shape[1]
    tokens, cot = forward_tokens[0], backward_cotangent[0]
    count = tokens.shape[0]
    f_ids, b_ids = forward_routes.reshape(1, count), backward_routes.reshape(1, count)
    f_gate, b_gate = forward_gates.reshape(1, count), backward_gates.reshape(1, count)
    slots = experts * SLOTS
    first = width * 3 // 16
    part = functools.partial
    blocks = ((slots, width), BF)

    packed = call(part(pack_kernel, experts, True), [blocks], b_ids, b_gate, cot, out_first=True)
    cot_rows = exchange(packed)
    factors = call(part(recompute_kernel, experts), [((slots, 2 * ff), F32)], x, w_gate, w_up)
    own, *others = call(quarters_kernel, [((rows, width // 4), BF)] * 4, x, in_hbm=True)
    others = [swap(other, flip + 1) for flip, other in enumerate(others)]
    x_t = call(
        transpose_kernel, [((width // 4, 4 * rows), BF)], own, others[1], others[0], others[2],
        scratch=[pltpu.VMEM((4 * rows, width // 4), BF)], in_hbm=True,
    )
    back, grads = call(
        part(backward_kernel, experts), [blocks, ((rows, 2 * ff), BF)],
        w_down, cot_rows, factors, w_gate, w_up, out_first=True, own_fetch=True,
    )
    back = exchange(back)

    near = [grads, swap(grads, 2)]
    keep, send = call(
        partial_kernel, [((width // 8, 2 * ff), F32), ((width // 8, 2 * ff), BF)],
        x_t, *near, swap(near[0], 1), swap(near[1], 1),
        scratch=[pltpu.VMEM((4 * rows, 2 * ff), BF)],
    )
    kept, send = call(
        halve_kernel, [((width // 16, 2 * ff), F32), ((width // 16, 2 * ff), BF)],
        keep, swap(send, 4),
    )
    weight_grads = call(last_kernel, [((width // 16, 2 * ff), BF)], kept, swap(send, 8))

    widths = (first, width - first)
    local = call(
        part(unpack_kernel, experts, False), [((count, some), BF) for some in widths],
        b_ids, b_gate, cot, back,
    )
    around = turn(turn(turn(local[0], 1), 1), 1)
    received = call(join_kernel, [((count, width), BF)], around, turn(local[1], -1))

    f_packed = call(part(pack_kernel, experts, False), [blocks], f_ids, f_gate, tokens, out_first=True)
    f_rows = exchange(f_packed)
    f_out = call(forward_kernel, [blocks], f_rows, w_gate, w_up, w_down, out_first=True)
    f_back = exchange(f_out)
    forward_out = call(part(unpack_kernel, experts, True), [((count, width), BF)], f_ids, f_gate, tokens, f_back)
    return forward_out[None], received[None], weight_grads[None, None]


def solution(mesh):
    token = P("section", ("expert", "replica"), None)
    weight = P("section", "expert", None, None)
    row = P("section", "expert", "replica", None)
    return jax.shard_map(
        shards,
        mesh=mesh,
        in_specs=(token,) * 6 + (row,) + (weight,) * 3,
        out_specs=(token, token, row),
        check_vma=False,
    )
```

```python
import functools

import jax
import jax.numpy as jnp
from jax import lax
from jax.experimental import pallas as pl
from jax.experimental.pallas import tpu as pltpu
from jax.sharding import PartitionSpec as P


BF = jnp.bfloat16
F32 = jnp.float32
SLOTS = 16
COLS = 512
PLAIN = (((1,), (0,)), ((), ()))
RIGHT_T = (((1,), (1,)), ((), ()))
LEFT_T = (((0,), (0,)), ((), ()))


def dot(a, b, dims=PLAIN):
    return lax.dot_general(a, b, dims, preferred_element_type=F32)


def iota(shape, axis):
    return lax.broadcasted_iota(jnp.int32, shape, axis)


def slot_mask(ids, experts):
    tokens = ids.shape[1]
    member = iota((experts, tokens), 0) == ids
    ones = jnp.where(member, 1.0, 0.0)
    before = jnp.where(iota((tokens, tokens), 0) < iota((tokens, tokens), 1), 1.0, 0.0)
    earlier = dot(ones.astype(BF), before.astype(BF))
    slot = jnp.sum(ones * earlier, axis=0, keepdims=True).astype(jnp.int32)
    return iota((experts * SLOTS, tokens), 0) == ids * SLOTS + slot


def columns(width):
    return [slice(at, min(at + COLS, width)) for at in range(0, width, COLS)]


def write_out(held_ref, out_ref, sem_ref, fill):
    copies = []
    for k, part in enumerate(columns(out_ref.shape[1])):
        held_ref[:, part] = fill(part)
        copies.append(pltpu.make_async_copy(held_ref.at[:, part], out_ref.at[:, part], sem_ref.at[k]))
        copies[-1].start()
    for copy in copies:
        copy.wait()


def pack_kernel(experts, scaled, ids_ref, gate_ref, value_ref, out_ref, held_ref, sem_ref):
    mask = slot_mask(ids_ref[...], experts)
    table = jnp.where(mask, 1.0, 0.0).astype(BF)
    if scaled:
        gate = jnp.sum(jnp.where(mask, gate_ref[...], 0.0), axis=1, keepdims=True)

    def fill(part):
        rows = dot(table, value_ref[:, part])
        return (rows * gate if scaled else rows).astype(BF)

    write_out(held_ref, out_ref, sem_ref, fill)


def unpack_kernel(experts, scaled, ids_ref, gate_ref, value_ref, back_ref, *out_refs):
    mask = slot_mask(ids_ref[...], experts)
    table = jnp.where(mask, 1.0, 0.0).astype(BF)
    tokens = ids_ref.shape[1]
    if scaled:
        eye = iota((tokens, tokens), 0) == iota((tokens, tokens), 1)
        gate = jnp.sum(jnp.where(eye, gate_ref[...], 0.0), axis=1, keepdims=True)
    at = 0
    for out_ref in out_refs:
        for part in columns(out_ref.shape[1]):
            source = slice(at + part.start, at + part.stop)
            rows = dot(table, back_ref[:, source], LEFT_T)
            if scaled:
                rows = rows * gate
            out_ref[:, part] = (value_ref[:, source].astype(F32) + rows).astype(BF)
        at += out_ref.shape[1]


def spread_mask(experts, rows):
    capacity = rows // experts
    shape = (experts * SLOTS, rows)
    at, of = iota(shape, 0), iota(shape, 1)
    filled = at % SLOTS < capacity
    return filled & (of == at // SLOTS * capacity + at % SLOTS)


def recompute_kernel(experts, x_ref, gate_ref, up_ref, factors_ref):
    ff = gate_ref.shape[1]
    table = jnp.where(spread_mask(experts, x_ref.shape[0]), 1.0, 0.0).astype(BF)
    rows = dot(table, x_ref[...]).astype(BF)
    gate_pre = dot(rows, gate_ref[...])
    up_pre = dot(rows, up_ref[...])
    sigma = jax.nn.sigmoid(gate_pre)
    factors_ref[:, ff:] = gate_pre * sigma
    factors_ref[:, :ff] = up_pre * sigma * (1.0 + gate_pre * (1.0 - sigma))


def backward_kernel(experts, *refs):
    sources, (out_ref, grads_ref, held_ref, sem_ref), (*inputs, in_sem_ref) = refs[:5], refs[5:9], refs[9:]
    fetches = [
        pltpu.make_async_copy(source, held, in_sem_ref.at[k])
        for k, (source, held) in enumerate(zip(sources, inputs))
    ]
    for fetch in fetches:
        fetch.start()
    down_ref, cot_ref, factors_ref, gate_ref, up_ref = inputs
    ff = gate_ref.shape[1]
    fetches[0].wait()
    fetches[1].wait()
    hidden_grad = dot(cot_ref[...], down_ref[...])
    fetches[2].wait()
    gate_grad = (hidden_grad * factors_ref[:, :ff]).astype(BF)
    up_grad = (hidden_grad * factors_ref[:, ff:]).astype(BF)
    table = jnp.where(spread_mask(experts, grads_ref.shape[0]), 1.0, 0.0).astype(BF)
    grads_ref[:, :ff] = dot(table, gate_grad, LEFT_T).astype(BF)
    grads_ref[:, ff:] = dot(table, up_grad, LEFT_T).astype(BF)
    fetches[3].wait()
    fetches[4].wait()

    def fill(part):
        grad = dot(gate_grad, gate_ref[part, :], RIGHT_T)
        return (grad + dot(up_grad, up_ref[part, :], RIGHT_T)).astype(BF)

    write_out(held_ref, out_ref, sem_ref, fill)


def forward_kernel(x_ref, gate_ref, up_ref, down_ref, out_ref, held_ref, sem_ref):
    gate_pre = dot(x_ref[...], gate_ref[...])
    up_pre = dot(x_ref[...], up_ref[...])
    hidden = (gate_pre * jax.nn.sigmoid(gate_pre) * up_pre).astype(BF)

    def fill(part):
        return dot(hidden, down_ref[part, :], RIGHT_T).astype(BF)

    write_out(held_ref, out_ref, sem_ref, fill)


def call(kernel, outs, *args, scratch=(), out_first=False, own_fetch=False, in_hbm=False):
    in_hbm = in_hbm or out_first
    shapes = [jax.ShapeDtypeStruct(*out) for out in outs]
    specs = [pl.BlockSpec() for _ in outs]
    if out_first:
        specs[0] = pl.BlockSpec(memory_space=pltpu.HBM)
        parts = len(columns(shapes[0].shape[1]))
        scratch = [pltpu.VMEM(*outs[0]), pltpu.SemaphoreType.DMA((parts,))]
    in_specs = [pl.BlockSpec(memory_space=pltpu.HBM) if own_fetch else pl.BlockSpec() for _ in args]
    if own_fetch:
        scratch += [pltpu.VMEM(x.shape, x.dtype) for x in args] + [pltpu.SemaphoreType.DMA((len(args),))]
    moved = sum(x.size * x.dtype.itemsize for x in list(args) + shapes)
    result = pl.pallas_call(
        kernel,
        out_shape=shapes,
        in_specs=in_specs,
        out_specs=specs,
        scratch_shapes=scratch,
        compiler_params=pltpu.CompilerParams(**({} if in_hbm else {"vmem_limit_bytes": 16 << 20})),
        cost_estimate=pl.CostEstimate(flops=0, bytes_accessed=moved, transcendentals=0),
    )(*args)
    return result[0] if len(outs) == 1 else result


def quarters_kernel(x_ref, *out_refs):
    mine = lax.rem(lax.axis_index("replica"), 4)
    for flip, out_ref in enumerate(out_refs):
        owner = mine ^ flip
        for k in range(out_ref.shape[1] // 128):
            at = pl.multiple_of((4 * k + owner) * 128, 128)
            out_ref[:, k * 128 : (k + 1) * 128] = x_ref[:, pl.ds(at, 128)]


def transpose_kernel(*refs):
    *x_refs, out_ref, cat_ref = refs
    rows = x_refs[0].shape[0]
    for k, x_ref in enumerate(x_refs):
        cat_ref[k * rows : (k + 1) * rows, :] = x_ref[...]
    for k in range(out_ref.shape[0] // 128):
        out_ref[k * 128 : (k + 1) * 128, :] = cat_ref[:, k * 128 : (k + 1) * 128].T


def partial_kernel(x_ref, *refs):
    grad_refs, keep_ref, send_refs, cat_ref = refs[:4], refs[4], refs[5:-1], refs[-1]
    rows = grad_refs[0].shape[0]
    for k, grad_ref in enumerate(grad_refs):
        cat_ref[k * rows : (k + 1) * rows, :] = grad_ref[...]
    place = lax.axis_index("replica") // 4
    for flip, out_ref in enumerate([keep_ref, *send_refs]):
        at = pl.multiple_of((place ^ flip) * 128, 128)
        out_ref[...] = dot(x_ref[pl.ds(at, 128), :], cat_ref[...]).astype(out_ref.dtype)


def total_kernel(keep_ref, *refs):
    *got_refs, out_ref = refs
    total = keep_ref[...]
    for got_ref in got_refs:
        total = total + got_ref[...].astype(F32)
    out_ref[...] = total.astype(BF)


def join_kernel(*refs):
    *part_refs, out_ref = refs
    at = 0
    for part_ref in part_refs:
        out_ref[:, at : at + part_ref.shape[1]] = part_ref[...]
        at += part_ref.shape[1]


def swap(value, bit):
    count = lax.axis_size("replica")
    return lax.ppermute(value, "replica", [(at, at ^ bit) for at in range(count)])


def turn(value, steps):
    count = lax.axis_size("section")
    return lax.ppermute(value, "section", [(at, (at + steps) % count) for at in range(count)])


def exchange(rows):
    experts = lax.axis_size("expert")
    blocks = rows.reshape(experts, SLOTS, rows.shape[1])
    got = lax.all_to_all(blocks, "expert", 0, 0, tiled=True)
    return got.reshape(rows.shape)


def shards(
    forward_tokens,
    forward_routes,
    forward_gates,
    backward_cotangent,
    backward_routes,
    backward_gates,
    saved_rows,
    gate_weight,
    up_weight,
    down_weight,
):
    experts = lax.axis_size("expert")
    x = saved_rows[0, 0]
    rows, width = x.shape
    w_gate, w_up, w_down = gate_weight[0, 0], up_weight[0, 0], down_weight[0, 0]
    ff = w_gate.shape[1]
    tokens, cot = forward_tokens[0], backward_cotangent[0]
    count = tokens.shape[0]
    f_ids, b_ids = forward_routes.reshape(1, count), backward_routes.reshape(1, count)
    f_gate, b_gate = forward_gates.reshape(1, count), backward_gates.reshape(1, count)
    slots = experts * SLOTS
    first = width * 3 // 16
    part = functools.partial
    blocks = ((slots, width), BF)

    packed = call(part(pack_kernel, experts, True), [blocks], b_ids, b_gate, cot, out_first=True)
    cot_rows = exchange(packed)
    factors = call(part(recompute_kernel, experts), [((slots, 2 * ff), F32)], x, w_gate, w_up)
    own, *others = call(quarters_kernel, [((rows, width // 4), BF)] * 4, x, in_hbm=True)
    others = [swap(other, flip + 1) for flip, other in enumerate(others)]
    x_t = call(
        transpose_kernel, [((width // 4, 4 * rows), BF)], own, others[1], others[0], others[2],
        scratch=[pltpu.VMEM((4 * rows, width // 4), BF)], in_hbm=True,
    )
    back, grads = call(
        part(backward_kernel, experts), [blocks, ((rows, 2 * ff), BF)],
        w_down, cot_rows, factors, w_gate, w_up, out_first=True, own_fetch=True,
    )
    back = exchange(back)

    near = [grads, swap(grads, 2)]
    block = (width // 16, 2 * ff)
    keep, *sends = call(
        partial_kernel, [(block, F32)] + [(block, BF)] * 3,
        x_t, *near, swap(near[0], 1), swap(near[1], 1),
        scratch=[pltpu.VMEM((4 * rows, 2 * ff), BF)],
    )
    got = [swap(send, 4 * (flip + 1)) for flip, send in enumerate(sends)]
    weight_grads = call(total_kernel, [(block, BF)], keep, *got)

    widths = (first, width - first)
    local = call(
        part(unpack_kernel, experts, False), [((count, some), BF) for some in widths],
        b_ids, b_gate, cot, back,
    )
    around = turn(turn(turn(local[0], 1), 1), 1)
    received = call(join_kernel, [((count, width), BF)], around, turn(local[1], -1))

    f_packed = call(part(pack_kernel, experts, False), [blocks], f_ids, f_gate, tokens, out_first=True)
    f_rows = exchange(f_packed)
    f_out = call(forward_kernel, [blocks], f_rows, w_gate, w_up, w_down, out_first=True)
    f_back = exchange(f_out)
    forward_out = call(part(unpack_kernel, experts, True), [((count, width), BF)], f_ids, f_gate, tokens, f_back)
    return forward_out[None], received[None], weight_grads[None, None]


def solution(mesh):
    token = P("section", ("expert", "replica"), None)
    weight = P("section", "expert", None, None)
    row = P("section", "expert", "replica", None)
    return jax.shard_map(
        shards,
        mesh=mesh,
        in_specs=(token,) * 6 + (row,) + (weight,) * 3,
        out_specs=(token, token, row),
        check_vma=False,
    )
```
